32 devices in a mesh: gx: 4 (over z), gy: 4 (over x, core), gz: 2 (over y).
Axes of the slice: x: 2, y: 2, z: 4, core: 2. Of those that a mesh axis runs over, the one named last changes fastest.
Arguments:
- features: float32 [4, 4, 2, 256, 256], P('gx', 'gy', 'gz'), may hold values from -6 to 6
- positions: float32 [4, 4, 2, 3, 256], P('gx', 'gy', 'gz'), may hold values from 0 to 1
- counts: int32 [4, 4, 2], P('gx', 'gy', 'gz'), may hold values from 51 to 256, as said below
- w_src: float32 [256, 256], replicated, may hold values from -0.375 to 0.375
- w_out: float32 [256, 256], replicated, may hold values from -0.375 to 0.375
- radial: float32 [8, 256], replicated, may hold values from -5 to 5
Outputs:
- updated: float32 [4, 4, 2, 256, 256], P('gx', 'gy', 'gz')
The draws below stay inside these ranges and needn't reach their ends.
Inputs may be any that keep to these rules, and one draw needn't show every extreme that they name: The atoms of a bin fill its first counts slots; some bin is full in every draw, and some bins hold more than 128 atoms.
All inputs are finite; a program needn't handle non-finite values.
Results may differ from the reference program's by a relative error of at most 0.0003.
Values sent between devices are 32-bit elements; how exact they have to be, the bound alone decides.
A program may use at most 64 MiB of HBM per device.

```python
import jax
import jax.numpy as jnp
from jax import lax

F = 256
NRBF = 8
CAP = 256
BLK = 128
BINS_X = 4
BINS_Y = 4
BINS_Z = 2


def draw_counts(key, part):
    key_light, key_dense, key_pick, key_spot = jax.random.split(jax.random.fold_in(key, 17), 4)
    grid_shape = (BINS_X, BINS_Y, BINS_Z)
    light_counts = jax.random.randint(key_light, grid_shape, CAP // 5, BLK + 1)
    dense_counts = jax.random.randint(key_dense, grid_shape, BLK + 1, CAP + 1)
    is_dense = jax.random.randint(key_pick, grid_shape, 0, 8) == 0
    values_flat = jnp.where(is_dense, dense_counts, light_counts).reshape(-1)
    full_bin = jax.random.randint(key_spot, (), 0, BINS_X * BINS_Y * BINS_Z)
    values_flat = jnp.where(jnp.arange(BINS_X * BINS_Y * BINS_Z) == full_bin, CAP, values_flat)
    return values_flat.reshape(grid_shape).astype(jnp.int32)


def steps_of(own_key, extent, pieces, smallest, top_value):
    def one(axis_at, blocks):
        steps = jax.random.uniform(jax.random.fold_in(jax.random.fold_in(own_key, 6), axis_at), (blocks,), jnp.float32, smallest / len(pieces), top_value / len(pieces))
        return jnp.repeat(jnp.exp(steps), extent[axis_at] // blocks).reshape((-1,) + (1,) * (len(extent) - axis_at - 1))

    level = one(*pieces[0])
    for cut in pieces[1:]:
        level = level * one(*cut)
    return level


def noise(rng, extent, scale, reach, cuts=(), held_as=jnp.bfloat16):
    loudness = steps_of(rng, extent, cuts, -0.22, 0.18) if cuts else 1.0
    result = jax.random.normal(rng, extent, jnp.float32) * scale * loudness
    return jnp.minimum(jnp.maximum(result, -reach), reach).astype(held_as)


def setup_inputs(seed: int = 0) -> dict:
    arg_keys = jax.random.split(jax.random.key(seed), 7)
    features = noise(arg_keys[0], (BINS_X, BINS_Y, BINS_Z, CAP, F), 1.0, 6.0, ((0, 4), (1, 4), (2, 2)), jnp.float32)
    positions = jnp.clip(1.0 * jax.random.uniform(arg_keys[1], (BINS_X, BINS_Y, BINS_Z, 3, CAP), jnp.float32) ** steps_of(arg_keys[1], (BINS_X, BINS_Y, BINS_Z, 3, CAP), ((0, 4), (1, 4), (2, 2)), -0.2, 0.2), 0.0, 1.0)
    counts = draw_counts(jax.random.fold_in(arg_keys[6], 71), 0)
    w_src = noise(arg_keys[3], (F, F), F ** -0.5, 0.375, (), jnp.float32)
    w_out = noise(arg_keys[4], (F, F), F ** -0.5, 0.375, (), jnp.float32)
    radial = noise(arg_keys[5], (NRBF, F), 1.0, 5.0, (), jnp.float32)
    return {"features": features, "positions": positions, "counts": counts, "w_src": w_src, "w_out": w_out, "radial": radial}


far_value = 100.0
gamma_width = 10.0
message_scale = 0.125
highest = lax.Precision.HIGHEST

def offset_of(task_index):
    return jnp.stack([task_index // 9, task_index // 3 % 3, task_index % 3]).astype(jnp.float32) - 1.0

def radial_terms(left_pos, right_pos, right_feats, offset, same_bin, row_block, col_block, radial):
    rows_left = lax.dynamic_slice_in_dim(left_pos, row_block * BLK, BLK, 1)
    rows_right = lax.dynamic_slice_in_dim(right_pos, col_block * BLK, BLK, 1) + offset[:, None]
    separation = rows_right[:, None, :] - rows_left[:, :, None]
    distance = jnp.sqrt(lax.optimization_barrier(jnp.sum(separation * separation, axis=0)))
    envelope = jnp.where(distance < 1.0, 0.5 * (jnp.cos(jnp.pi * distance) + 1.0), 0.0)
    diagonal = lax.broadcasted_iota(jnp.int32, (BLK, BLK), 0) == lax.broadcasted_iota(jnp.int32, (BLK, BLK), 1)
    envelope = jnp.where(diagonal & same_bin & (row_block == col_block), 0.0, envelope)
    centres = (lax.broadcasted_iota(jnp.float32, (1, NRBF, 1), 1) + 0.5) / NRBF
    radial_basis = envelope[:, None, :] * jnp.exp(-gamma_width * (distance[:, None, :] - centres) ** 2)
    feature_rows = lax.dynamic_slice_in_dim(right_feats, col_block * BLK, BLK, 0)
    weighted = (radial[:, None, :] * feature_rows[None, :, :]).reshape(NRBF * BLK, feature_rows.shape[1])
    return jnp.dot(radial_basis.reshape(BLK, NRBF * BLK), weighted, precision=highest, preferred_element_type=jnp.float32)

def task_sum(left_pos, right_pos, right_feats, offset, same_bin, left_blocks, right_blocks, radial, running):
    divisor = jnp.maximum(right_blocks, 1)

    def add_pair(counter, partial_sum):
        row_block = counter // divisor
        col_block = counter % divisor
        term = radial_terms(left_pos, right_pos, right_feats, offset, same_bin, row_block, col_block, radial)
        current = lax.dynamic_slice_in_dim(partial_sum, row_block * BLK, BLK, 0)
        return lax.dynamic_update_slice_in_dim(partial_sum, current + term, row_block * BLK, 0)
    return lax.fori_loop(0, left_blocks * right_blocks, add_pair, running)

def reference(features, positions, counts, w_src, w_out, radial):
    bin_total = BINS_X * BINS_Y * BINS_Z
    width = features.shape[-1]
    flat_feats = features.reshape(bin_total * CAP, width)
    projected = jnp.dot(flat_feats, w_src, precision=highest, preferred_element_type=jnp.float32)
    projected = projected.reshape(BINS_X, BINS_Y, BINS_Z, CAP, width)
    slot_index = jnp.arange(CAP, dtype=jnp.int32)
    placed = jnp.where(slot_index[None, None, None, None, :] < counts[:, :, :, None, None], positions, far_value)
    blocks = (counts + BLK - 1) // BLK

    def bin_message(bin_index):
        coord_x = bin_index // (BINS_Y * BINS_Z)
        coord_y = bin_index // BINS_Z % BINS_Y
        coord_z = bin_index % BINS_Z

        def add_task(task_index, running):
            near_x = (coord_x + task_index // 9 - 1) % BINS_X
            near_y = (coord_y + task_index // 3 % 3 - 1) % BINS_Y
            near_z = (coord_z + task_index % 3 - 1) % BINS_Z
            return task_sum(placed[coord_x, coord_y, coord_z], placed[near_x, near_y, near_z], projected[near_x, near_y, near_z], offset_of(task_index), task_index == 13, blocks[coord_x, coord_y, coord_z], blocks[near_x, near_y, near_z], radial, running)
        return lax.fori_loop(0, 27, add_task, jnp.zeros((CAP, width), jnp.float32))
    message = lax.map(bin_message, jnp.arange(bin_total, dtype=jnp.int32))
    mixed = jnp.dot(message_scale * message.reshape(bin_total * CAP, width), w_out, precision=highest, preferred_element_type=jnp.float32)
    return (flat_feats + jax.nn.silu(mixed)).reshape(features.shape)
```

```python
import math

import jax
import jax.numpy as jnp
import numpy as np
from jax import lax
from jax.experimental import pallas as pl
from jax.experimental.pallas import tpu as pltpu
from jax.sharding import PartitionSpec as P

BLK = 128
CHUNK = 256
far_value = 100.0
gamma_width = 10.0
message_scale = 0.125
highest = lax.Precision.HIGHEST
f32, bf16, i32 = jnp.float32, jnp.bfloat16, jnp.int32


def envelope_coefficients():
    t = np.cos(np.pi * (np.arange(64) + 0.5) / 64) * 0.5 + 0.5
    value = 0.5 * (np.cos(np.pi * np.sqrt(t)) + 1.0)
    fit = np.polynomial.chebyshev.Chebyshev.fit(t, value, 7, domain=[0, 1])
    return [float(c) for c in fit.convert(kind=np.polynomial.Polynomial).coef]


ENVELOPE = envelope_coefficients()


def split(value):
    high = value.astype(bf16)
    return high, (value - high.astype(f32)).astype(bf16)


def dot(a, b):
    return jnp.dot(a, b, preferred_element_type=f32)


def dot3(a, b):
    ah, al = split(a)
    bh, bl = split(b)
    return dot(ah, bh) + (dot(ah, bl) + dot(al, bh))


def project_kernel(feats_ref, place_ref, w_ref, early_ref, later_ref):
    value = dot3(feats_ref[...], w_ref[...])
    early_ref[:BLK] = value[:BLK]
    early_ref[BLK:] = place_ref[...]
    later_ref[...] = value[BLK:]


def pairs_kernel(tiles, mirrored, nrbf, *refs):
    early = refs[:tiles]
    later = refs[tiles : 2 * tiles]
    shift_ref, own_ref, feats_ref, radial_ref, w_ref, out_ref = refs[2 * tiles : 2 * tiles + 6]
    high_p, low_p, where_j, where_i, high_b, low_b, total, message = refs[2 * tiles + 6 :]
    lane = lax.broadcasted_iota(i32, (8, BLK), 1)
    counts = [jnp.max(t[BLK + 3 : BLK + 4, :BLK]).astype(i32) for t in early]
    own_blocks = (counts[0] + BLK - 1) // BLK

    def append(rows_ref, place, count, at):
        rows = (count + 15) // 16 * 16
        high, low = split(rows_ref[:BLK])
        at = pl.multiple_of(at, 16)
        high_p[pl.ds(at, BLK), :] = high
        low_p[pl.ds(at, BLK), :] = low
        turn = lax.rem(at, BLK)
        page = at // BLK
        rolled = pltpu.roll(place, turn, 1)
        where_j[page] = jnp.where(lane >= turn, rolled, where_j[page])
        where_j[page + 1] = rolled
        return at + rows

    at = jnp.int32(0)
    for half, source in ((0, early), (1, later)):
        for t in range(tiles):
            count = own_blocks * BLK if t == 0 else counts[t]
            here = jnp.clip(count - half * BLK, 0, BLK)
            place = early[t][BLK:, half * BLK : (half + 1) * BLK]
            shift = shift_ref[t]
            if half:
                @pl.when(here > 0)
                def _():
                    append(source[t], place + shift, here, at)

                at = at + (here + 15) // 16 * 16
            else:
                at = append(source[t], place + shift, here, at)
            if t == 0 and half == 0 and tiles:
                @pl.when(own_blocks > 1)
                def _():
                    append(later[0], early[0][BLK:, BLK:] + shift_ref[0], jnp.int32(BLK), jnp.int32(BLK))

                at = own_blocks * BLK
                counts[0] = jnp.int32(0)
                own_count = own_blocks
                own_blocks = jnp.int32(0)
    own_blocks = own_count
    tail = pl.multiple_of(at, 16)
    zeros = jnp.zeros((CHUNK, high_p.shape[1]), bf16)
    high_p[pl.ds(tail, CHUNK), :] = zeros
    low_p[pl.ds(tail, CHUNK), :] = zeros
    far = jnp.where(lax.broadcasted_iota(i32, (8, BLK), 0) < 4, 2 * far_value, 0.0)
    page = at // BLK
    where_j[page] = jnp.where(lane >= lax.rem(at, BLK), far, where_j[page])
    where_j[page + 1] = far
    where_j[page + 2] = far
    chunks = (at + CHUNK - 1) // CHUNK
    place_i = own_ref[...]
    difference = lax.broadcasted_iota(i32, (32, BLK), 0) - lax.broadcasted_iota(i32, (32, BLK), 1)

    message[...] = jnp.zeros_like(message)

    @pl.loop(0, own_blocks)
    def _(row_block):
        row = pl.multiple_of(row_block * BLK, BLK)
        mine = own_ref[pl.ds(row, BLK), :]
        for c in range(3):
            where_i[c] = jnp.broadcast_to(mine[:, c : c + 1], (BLK, BLK))
        total[...] = jnp.zeros_like(total)

        @pl.loop(0, chunks)
        def _(chunk):
            for half in range(CHUNK // BLK):
                theirs = where_j[chunk * (CHUNK // BLK) + half]
                gap = chunk * CHUNK + half * BLK - row
                for sub in range(0, BLK, 32):
                    square = None
                    for c in range(3):
                        delta = theirs[c : c + 1, :] - where_i[c, sub : sub + 32, :]
                        if mirrored[c]:
                            delta = theirs[c + 4 : c + 5, :] - jnp.abs(delta)
                        delta = delta * delta
                        square = delta if square is None else square + delta
                    reach = (square < 1.0) & (difference != gap - sub)
                    square = jnp.minimum(square, 1.0)
                    distance = square * lax.rsqrt(jnp.maximum(square, 1e-30))
                    envelope = jnp.full_like(square, ENVELOPE[-1])
                    for coefficient in ENVELOPE[-2::-1]:
                        envelope = envelope * square + coefficient
                    envelope = jnp.where(reach, envelope, 0.0)
                    step = gamma_width / nrbf
                    basis = envelope * jnp.exp(step * distance - gamma_width * square)
                    ratio = jnp.exp(2.0 * step * distance)
                    for k in range(nrbf):
                        if k:
                            basis = basis * ratio
                        high, low = split(basis)
                        spot = (slice(k * BLK + sub, k * BLK + sub + 32), slice(half * BLK, half * BLK + BLK))
                        high_b[spot] = high
                        low_b[spot] = low
            base = pl.multiple_of(chunk * CHUNK, CHUNK)
            ph = high_p[pl.ds(base, CHUNK), :]
            pw = low_p[pl.ds(base, CHUNK), :]
            bh = high_b[...]
            total[...] += dot(bh, ph) + (dot(bh, pw) + dot(low_b[...], ph))

        value = None
        for k in range(nrbf):
            weight = radial_ref[k : k + 1, :] * math.exp(-gamma_width * ((k + 0.5) / nrbf) ** 2)
            term = total[k * BLK : (k + 1) * BLK, :] * weight
            value = term if value is None else value + term
        message[pl.ds(row, BLK), :] = value * message_scale

    mixed = dot3(message[...], w_ref[...])
    out_ref[...] = feats_ref[...] + mixed / (1.0 + jnp.exp(-mixed))


def exchange(values, axis, pairs):
    return [tuple(lax.ppermute(v, axis, pairs) for v in value) for value in values]


def near_tiles(own, names):
    ax, ay, az = names
    tiles = [(own, [0, 0, 0], [0, 0, 0])]

    def moved(which, dim, pairs, offset, mirror):
        arrays = exchange([w[0] for w in which], names[dim], pairs)
        found = []
        for a, (_, o, m) in zip(arrays, which):
            o, m = list(o), list(m)
            if mirror:
                m[dim] = 1
            else:
                o[dim] = offset
            found.append((a, o, m))
        return found

    def grow(which, dim):
        n = lax.axis_size(names[dim])
        if n == 2:
            return moved(which, dim, [(0, 1), (1, 0)], 0, True)
        up = [(i, (i + 1) % n) for i in range(n)]
        down = [((i + 1) % n, i) for i in range(n)]
        return moved(which, dim, up, -1, False) + moved(which, dim, down, 1, False)

    n = lax.axis_size(ay)
    paired = n > 2 and n % 2 == 0
    if paired:
        side = 1 - 2 * lax.rem(lax.axis_index(ay), 2)
        cross = [(i, (i - 1) % n if i % 2 == 0 else (i + 1) % n) for i in range(n)]
        partner = [(i, i ^ 1) for i in range(n)]
        tiles = tiles + moved(tiles, 1, cross, -side, False)
    else:
        tiles = tiles + grow(tiles, 1)
    tiles = tiles + grow(tiles, 2)
    tiles = tiles + grow(tiles, 0)
    if paired:
        middle = [t for t in tiles if isinstance(t[1][1], int) and t[1][1] == 0]
        tiles = tiles + moved(middle, 1, partner, side, False)
    return tiles


def local(features, positions, counts, w_src, w_out, radial):
    feats = features[0, 0, 0]
    cap, width = feats.shape
    nrbf = radial.shape[0]
    slot = lax.broadcasted_iota(i32, (1, cap), 1)
    count = counts[0, 0, 0]
    placed = jnp.where(slot < count, positions[0, 0, 0], far_value)
    place = jnp.concatenate([placed, jnp.broadcast_to(count.astype(f32), (1, cap)), jnp.zeros((4, cap), f32)])
    names = ("gx", "gy", "gz")
    early, later = pl.pallas_call(
        project_kernel,
        out_shape=(jax.ShapeDtypeStruct((BLK + 8, width), f32), jax.ShapeDtypeStruct((cap - BLK, width), f32)),
    )(feats, place, w_src)
    tiles = near_tiles((early, later), names)
    total = len(tiles)
    mirrored = tuple(lax.axis_size(n) == 2 for n in names)
    rows = []
    for _, offset, mirror in tiles:
        rows += [*offset, 0, *mirror, 0]
    shift = jnp.stack([jnp.asarray(r, f32) for r in rows]).reshape(total, 8, 1)
    shift = jnp.broadcast_to(shift, (total, 8, BLK))
    own = jnp.concatenate([placed.T, jnp.zeros((cap, 5), f32)], axis=1)
    room = total * cap + 2 * CHUNK
    out = pl.pallas_call(
        lambda *refs: pairs_kernel(total, mirrored, nrbf, *refs),
        out_shape=jax.ShapeDtypeStruct((cap, width), f32),
        scratch_shapes=[
            pltpu.VMEM((room, width), bf16),
            pltpu.VMEM((room, width), bf16),
            pltpu.VMEM((room // BLK + 2, 8, BLK), f32),
            pltpu.VMEM((3, BLK, BLK), f32),
            pltpu.VMEM((nrbf * BLK, CHUNK), bf16),
            pltpu.VMEM((nrbf * BLK, CHUNK), bf16),
            pltpu.VMEM((nrbf * BLK, width), f32),
            pltpu.VMEM((cap, width), f32),
        ],
        compiler_params=pltpu.CompilerParams(vmem_limit_bytes=56 << 20),
    )(*[t[0][0] for t in tiles], *[t[0][1] for t in tiles], shift, own, feats, radial, w_out)
    return out[None, None, None]


def solution(mesh):
    in_specs = (P("gx", "gy", "gz", None, None), P("gx", "gy", "gz", None, None), P("gx", "gy", "gz"), P(), P(), P())
    return jax.shard_map(local, mesh=mesh, in_specs=in_specs, out_specs=P("gx", "gy", "gz", None, None), check_vma=False)
```

```python
import math

import jax
import jax.numpy as jnp
import numpy as np
from jax import lax
from jax.experimental import pallas as pl
from jax.experimental.pallas import tpu as pltpu
from jax.sharding import PartitionSpec as P

BLK = 128
CHUNK = 256
far_value = 100.0
gamma_width = 10.0
message_scale = 0.125
highest = lax.Precision.HIGHEST
f32, bf16, i32 = jnp.float32, jnp.bfloat16, jnp.int32


def envelope_coefficients():
    t = np.cos(np.pi * (np.arange(64) + 0.5) / 64) * 0.5 + 0.5
    value = 0.5 * (np.cos(np.pi * np.sqrt(t)) + 1.0)
    fit = np.polynomial.chebyshev.Chebyshev.fit(t, value, 7, domain=[0, 1])
    return [float(c) for c in fit.convert(kind=np.polynomial.Polynomial).coef]


ENVELOPE = envelope_coefficients()


def split(value):
    high = value.astype(bf16)
    return high, (value - high.astype(f32)).astype(bf16)


def dot(a, b):
    return jnp.dot(a, b, preferred_element_type=f32)


def dot3(a, b):
    ah, al = split(a)
    bh, bl = split(b)
    return dot(ah, bh) + (dot(ah, bl) + dot(al, bh))


def project_kernel(feats_ref, place_ref, w_ref, early_ref, later_ref):
    value = dot3(feats_ref[...], w_ref[...])
    early_ref[:BLK] = value[:BLK]
    early_ref[BLK:] = place_ref[...]
    later_ref[...] = value[BLK:]


def pairs_kernel(tiles, mirrored, nrbf, *refs):
    early_ref, later_ref, all_early, all_later, shift_ref, own_ref, feats_ref, radial_ref, w_ref, out_ref = refs[:10]
    high_p, low_p, where_j, where_i, high_b, low_b, total, message = refs[10:]
    early = [early_ref] + [all_early.at[t] for t in range(tiles - 1)]
    later = [later_ref] + [all_later.at[t] for t in range(tiles - 1)]
    lane = lax.broadcasted_iota(i32, (8, BLK), 1)
    counts = [jnp.max(t[BLK + 3 : BLK + 4, :BLK]).astype(i32) for t in early]
    own_blocks = (counts[0] + BLK - 1) // BLK

    def append(rows_ref, place, count, at):
        rows = (count + 15) // 16 * 16
        high, low = split(rows_ref[:BLK])
        at = pl.multiple_of(at, 16)
        high_p[pl.ds(at, BLK), :] = high
        low_p[pl.ds(at, BLK), :] = low
        turn = lax.rem(at, BLK)
        page = at // BLK
        rolled = pltpu.roll(place, turn, 1)
        where_j[page] = jnp.where(lane >= turn, rolled, where_j[page])
        where_j[page + 1] = rolled
        return at + rows

    at = jnp.int32(0)
    for half, source in ((0, early), (1, later)):
        for t in range(tiles):
            count = own_blocks * BLK if t == 0 else counts[t]
            here = jnp.clip(count - half * BLK, 0, BLK)
            place = early[t][BLK:, half * BLK : (half + 1) * BLK]
            shift = shift_ref[t]
            if half:
                @pl.when(here > 0)
                def _():
                    append(source[t], place + shift, here, at)

                at = at + (here + 15) // 16 * 16
            else:
                at = append(source[t], place + shift, here, at)
            if t == 0 and half == 0:
                @pl.when(own_blocks > 1)
                def _():
                    append(later[0], early[0][BLK:, BLK:] + shift_ref[0], jnp.int32(BLK), jnp.int32(BLK))

                at = own_blocks * BLK
                counts[0] = jnp.int32(0)
                own_count = own_blocks
                own_blocks = jnp.int32(0)
    own_blocks = own_count
    tail = pl.multiple_of(at, 16)
    zeros = jnp.zeros((CHUNK, high_p.shape[1]), bf16)
    high_p[pl.ds(tail, CHUNK), :] = zeros
    low_p[pl.ds(tail, CHUNK), :] = zeros
    far = jnp.where(lax.broadcasted_iota(i32, (8, BLK), 0) < 4, 2 * far_value, 0.0)
    page = at // BLK
    where_j[page] = jnp.where(lane >= lax.rem(at, BLK), far, where_j[page])
    where_j[page + 1] = far
    where_j[page + 2] = far
    chunks = (at + CHUNK - 1) // CHUNK
    difference = lax.broadcasted_iota(i32, (32, BLK), 0) - lax.broadcasted_iota(i32, (32, BLK), 1)

    message[...] = jnp.zeros_like(message)

    @pl.loop(0, own_blocks)
    def _(row_block):
        row = pl.multiple_of(row_block * BLK, BLK)
        mine = own_ref[pl.ds(row, BLK), :]
        for c in range(3):
            where_i[c] = jnp.broadcast_to(mine[:, c : c + 1], (BLK, BLK))
        total[...] = jnp.zeros_like(total)

        @pl.loop(0, chunks)
        def _(chunk):
            for half in range(CHUNK // BLK):
                theirs = where_j[chunk * (CHUNK // BLK) + half]
                gap = chunk * CHUNK + half * BLK - row
                for sub in range(0, BLK, 32):
                    square = None
                    for c in range(3):
                        delta = theirs[c : c + 1, :] - where_i[c, sub : sub + 32, :]
                        if mirrored[c]:
                            delta = theirs[c + 4 : c + 5, :] - jnp.abs(delta)
                        delta = delta * delta
                        square = delta if square is None else square + delta
                    reach = (square < 1.0) & (difference != gap - sub)
                    square = jnp.minimum(square, 1.0)
                    distance = square * lax.rsqrt(jnp.maximum(square, 1e-30))
                    envelope = jnp.full_like(square, ENVELOPE[-1])
                    for coefficient in ENVELOPE[-2::-1]:
                        envelope = envelope * square + coefficient
                    envelope = jnp.where(reach, envelope, 0.0)
                    step = gamma_width / nrbf
                    basis = envelope * jnp.exp(step * distance - gamma_width * square)
                    ratio = jnp.exp(2.0 * step * distance)
                    for k in range(nrbf):
                        if k:
                            basis = basis * ratio
                        high, low = split(basis)
                        spot = (slice(k * BLK + sub, k * BLK + sub + 32), slice(half * BLK, half * BLK + BLK))
                        high_b[spot] = high
                        low_b[spot] = low
            base = pl.multiple_of(chunk * CHUNK, CHUNK)
            ph = high_p[pl.ds(base, CHUNK), :]
            pw = low_p[pl.ds(base, CHUNK), :]
            bh = high_b[...]
            total[...] += dot(bh, ph) + (dot(bh, pw) + dot(low_b[...], ph))

        value = None
        for k in range(nrbf):
            weight = radial_ref[k : k + 1, :] * math.exp(-gamma_width * ((k + 0.5) / nrbf) ** 2)
            term = total[k * BLK : (k + 1) * BLK, :] * weight
            value = term if value is None else value + term
        message[pl.ds(row, BLK), :] = value * message_scale

    mixed = dot3(message[...], w_ref[...])
    out_ref[...] = feats_ref[...] + mixed / (1.0 + jnp.exp(-mixed))


def near_slots(sizes):
    kinds = []
    for axis, n in enumerate(sizes):
        if n == 2:
            kinds.append(("swap",))
        elif axis == 1 and n % 2 == 0:
            kinds.append(("cross", "partner"))
        else:
            kinds.append(("up", "down"))
    counts = [len(k) + 1 for k in kinds]
    slots = [(a, b, c) for a in range(counts[0]) for b in range(counts[1]) for c in range(counts[2])]
    return kinds, slots[1:]


def slot_offset(kind, index):
    side = 1 - 2 * lax.rem(index, 2)
    return {"swap": (0, 1), "cross": (-side, 0), "partner": (side, 0), "up": (-1, 0), "down": (1, 0)}[kind]


def routes(kinds):
    every = [[(axis, m) for m in range(len(kinds[axis]))] for axis in range(3)]
    first, last = every[1][:1], every[1][1:]
    return [
        [first, every[2], every[0], last],
        [first, every[0], every[2], last],
        [first, every[2], every[0], last],
        [every[2], every[0], every[1]],
    ]


def halo_kernel(names, sizes, early_ref, later_ref, all_early, all_later, send_sem, recv_sem):
    kinds, slots = near_slots(sizes)
    width = early_ref.shape[1]
    half = width // 2
    places = [lax.axis_index(n) for n in names]

    def target(axis, m):
        n, at = sizes[axis], places[axis]
        side = 1 - 2 * lax.rem(at, 2)
        step = {"swap": 1, "cross": n - side, "partner": n + side, "up": 1, "down": n - 1}[kinds[axis][m]]
        return {names[axis]: lax.rem(at + step, n)}

    moves = [(axis, m) for axis in range(3) for m in range(len(kinds[axis]))]
    barrier = pltpu.get_barrier_semaphore()
    for move in moves:
        pl.semaphore_signal(barrier, inc=1, device_id=target(*move), device_id_type=pl.DeviceIdType.MESH)
    pl.semaphore_wait(barrier, len(moves))

    def piece(slot, number):
        own = (early_ref, later_ref)[number // 2]
        full = own if slot is None else (all_early, all_later)[number // 2].at[slot]
        return full.at[:, pl.ds(number % 2 * half, half)]

    held = [[(0, 0, 0)] for _ in range(4)]
    stages = routes(kinds)
    copies, arrived = {}, set()

    def arrive(slot, number):
        if slot != (0, 0, 0) and (slot, number) not in arrived:
            arrived.add((slot, number))
            copies[slot, number].wait_recv()

    for stage in range(max(len(r) for r in stages)):
        fresh = [[] for _ in range(4)]
        for number in range(4):
            if stage >= len(stages[number]):
                continue
            for source in held[number]:
                for axis, m in stages[number][stage]:
                    if source[axis] != 0:
                        continue
                    arrive(source, number)
                    goal = tuple(m + 1 if d == axis else source[d] for d in range(3))
                    to = slots.index(goal)
                    origin = None if source == (0, 0, 0) else slots.index(source)
                    copy = pltpu.make_async_remote_copy(
                        src_ref=piece(origin, number),
                        dst_ref=piece(to, number),
                        send_sem=send_sem.at[to, number],
                        recv_sem=recv_sem.at[to, number],
                        device_id=target(axis, m),
                        device_id_type=pl.DeviceIdType.MESH,
                    )
                    copy.start()
                    copies[goal, number] = copy
                    fresh[number].append(goal)
        for number in range(4):
            held[number] += fresh[number]
    for (slot, number), copy in copies.items():
        arrive(slot, number)
        copy.wait_send()


def local(features, positions, counts, w_src, w_out, radial):
    feats = features[0, 0, 0]
    cap, width = feats.shape
    nrbf = radial.shape[0]
    slot = lax.broadcasted_iota(i32, (1, cap), 1)
    count = counts[0, 0, 0]
    placed = jnp.where(slot < count, positions[0, 0, 0], far_value)
    place = jnp.concatenate([placed, jnp.broadcast_to(count.astype(f32), (1, cap)), jnp.zeros((4, cap), f32)])
    names = ("gx", "gy", "gz")
    early, later = pl.pallas_call(
        project_kernel,
        out_shape=(jax.ShapeDtypeStruct((BLK + 8, width), f32), jax.ShapeDtypeStruct((cap - BLK, width), f32)),
    )(feats, place, w_src)
    sizes = tuple(lax.axis_size(n) for n in names)
    kinds, slots = near_slots(sizes)
    near = len(slots)
    total = near + 1
    all_early, all_later = pl.pallas_call(
        lambda *refs: halo_kernel(names, sizes, *refs),
        out_shape=(jax.ShapeDtypeStruct((near, *early.shape), f32), jax.ShapeDtypeStruct((near, *later.shape), f32)),
        in_specs=[pl.BlockSpec(memory_space=pl.ANY)] * 2,
        out_specs=(pl.BlockSpec(memory_space=pl.ANY),) * 2,
        scratch_shapes=[pltpu.SemaphoreType.DMA((near, 4)), pltpu.SemaphoreType.DMA((near, 4))],
        compiler_params=pltpu.CompilerParams(collective_id=0, has_side_effects=True),
    )(early, later)
    mirrored = tuple(n == 2 for n in sizes)
    rows = [0] * 8
    for slot in slots:
        found = [slot_offset(kinds[d][slot[d] - 1], lax.axis_index(names[d])) if slot[d] else (0, 0) for d in range(3)]
        rows += [*(f[0] for f in found), 0, *(f[1] for f in found), 0]
    shift = jnp.stack([jnp.asarray(r, f32) for r in rows]).reshape(total, 8, 1)
    shift = jnp.broadcast_to(shift, (total, 8, BLK))
    own = jnp.concatenate([placed.T, jnp.zeros((cap, 5), f32)], axis=1)
    room = total * cap + 2 * CHUNK
    out = pl.pallas_call(
        lambda *refs: pairs_kernel(total, mirrored, nrbf, *refs),
        out_shape=jax.ShapeDtypeStruct((cap, width), f32),
        scratch_shapes=[
            pltpu.VMEM((room, width), bf16),
            pltpu.VMEM((room, width), bf16),
            pltpu.VMEM((room // BLK + 2, 8, BLK), f32),
            pltpu.VMEM((3, BLK, BLK), f32),
            pltpu.VMEM((nrbf * BLK, CHUNK), bf16),
            pltpu.VMEM((nrbf * BLK, CHUNK), bf16),
            pltpu.VMEM((nrbf * BLK, width), f32),
            pltpu.VMEM((cap, width), f32),
        ],
        compiler_params=pltpu.CompilerParams(vmem_limit_bytes=56 << 20),
    )(early, later, all_early, all_later, shift, own, feats, radial, w_out)
    return out[None, None, None]


def solution(mesh):
    in_specs = (P("gx", "gy", "gz", None, None), P("gx", "gy", "gz", None, None), P("gx", "gy", "gz"), P(), P(), P())
    return jax.shard_map(local, mesh=mesh, in_specs=in_specs, out_specs=P("gx", "gy", "gz", None, None), check_vma=False)
```

```python
import math

import jax
import jax.numpy as jnp
import numpy as np
from jax import lax
from jax.experimental import pallas as pl
from jax.experimental.pallas import tpu as pltpu
from jax.sharding import PartitionSpec as P

BLK = 128
CHUNK = 256
far_value = 100.0
gamma_width = 10.0
message_scale = 0.125
highest = lax.Precision.HIGHEST
f32, bf16, i32 = jnp.float32, jnp.bfloat16, jnp.int32


def envelope_coefficients():
    t = np.cos(np.pi * (np.arange(64) + 0.5) / 64) * 0.5 + 0.5
    value = 0.5 * (np.cos(np.pi * np.sqrt(t)) + 1.0)
    fit = np.polynomial.chebyshev.Chebyshev.fit(t, value, 7, domain=[0, 1])
    return [float(c) for c in fit.convert(kind=np.polynomial.Polynomial).coef]


ENVELOPE = envelope_coefficients()


def split(value):
    high = value.astype(bf16)
    return high, (value - high.astype(f32)).astype(bf16)


def dot(a, b):
    return jnp.dot(a, b, preferred_element_type=f32)


def dot3(a, b):
    ah, al = split(a)
    bh, bl = split(b)
    return dot(ah, bh) + (dot(ah, bl) + dot(al, bh))


def project_kernel(count_ref, feats_ref, place_ref, w_ref, early_ref, later_ref):
    value = dot3(feats_ref[...], w_ref[...])
    cap = feats_ref.shape[0]
    count = count_ref[0]
    slot = lax.broadcasted_iota(i32, (1, cap), 1)
    early_ref[:BLK] = value[:BLK]
    early_ref[BLK : BLK + 3] = jnp.where(slot < count, place_ref[...], far_value)
    early_ref[BLK + 3 : BLK + 4] = jnp.broadcast_to(count.astype(f32), (1, cap))
    early_ref[BLK + 4 :] = jnp.zeros((4, cap), f32)
    later_ref[...] = value[BLK:]


def pairs_kernel(names, sizes, nrbf, *refs):
    kinds, slots = near_slots(sizes)
    tiles = len(slots) + 1
    mirrored = tuple(n == 2 for n in sizes)
    early_ref, later_ref, all_early, all_later, feats_ref, radial_ref, w_ref, out_ref = refs[:8]
    high_p, low_p, where_j, where_i, high_b, low_b, total, message = refs[8:]
    early = [early_ref] + [all_early.at[t] for t in range(tiles - 1)]
    later = [later_ref] + [all_later.at[t] for t in range(tiles - 1)]
    lane = lax.broadcasted_iota(i32, (8, BLK), 1)
    line = lax.broadcasted_iota(i32, (8, BLK), 0)
    places = [lax.axis_index(n) for n in names]

    def shift_of(t):
        shift = jnp.zeros((8, BLK), f32)
        for d in range(3):
            if t and slots[t - 1][d]:
                offset, mirror = slot_offset(kinds[d][slots[t - 1][d] - 1], places[d])
                shift = jnp.where(line == d, jnp.asarray(offset, i32).astype(f32), shift)
                shift = jnp.where(line == d + 4, float(mirror), shift)
        return shift

    counts = [jnp.max(t[BLK + 3 : BLK + 4, :BLK]).astype(i32) for t in early]
    own_blocks = (counts[0] + BLK - 1) // BLK

    def append(rows_ref, place, count, at):
        rows = (count + 15) // 16 * 16
        high, low = split(rows_ref[:BLK])
        at = pl.multiple_of(at, 16)
        high_p[pl.ds(at, BLK), :] = high
        low_p[pl.ds(at, BLK), :] = low
        turn = lax.rem(at, BLK)
        page = at // BLK
        rolled = pltpu.roll(place, turn, 1)
        where_j[page] = jnp.where(lane >= turn, rolled, where_j[page])
        where_j[page + 1] = rolled
        return at + rows

    at = jnp.int32(0)
    for half, source in ((0, early), (1, later)):
        for t in range(tiles):
            count = own_blocks * BLK if t == 0 else counts[t]
            here = jnp.clip(count - half * BLK, 0, BLK)
            place = early[t][BLK:, half * BLK : (half + 1) * BLK]
            shift = shift_of(t)
            if half:
                @pl.when(here > 0)
                def _():
                    append(source[t], place + shift, here, at)

                at = at + (here + 15) // 16 * 16
            else:
                at = append(source[t], place + shift, here, at)
            if t == 0 and half == 0:
                @pl.when(own_blocks > 1)
                def _():
                    append(later[0], early[0][BLK:, BLK:], jnp.int32(BLK), jnp.int32(BLK))

                at = own_blocks * BLK
                counts[0] = jnp.int32(0)
                own_count = own_blocks
                own_blocks = jnp.int32(0)
    own_blocks = own_count
    tail = pl.multiple_of(at, 16)
    zeros = jnp.zeros((CHUNK, high_p.shape[1]), bf16)
    high_p[pl.ds(tail, CHUNK), :] = zeros
    low_p[pl.ds(tail, CHUNK), :] = zeros
    far = jnp.where(line < 4, 2 * far_value, 0.0)
    page = at // BLK
    where_j[page] = jnp.where(lane >= lax.rem(at, BLK), far, where_j[page])
    where_j[page + 1] = far
    where_j[page + 2] = far
    chunks = (at + CHUNK - 1) // CHUNK
    difference = lax.broadcasted_iota(i32, (32, BLK), 0) - lax.broadcasted_iota(i32, (32, BLK), 1)

    message[...] = jnp.zeros_like(message)

    @pl.loop(0, own_blocks)
    def _(row_block):
        row = pl.multiple_of(row_block * BLK, BLK)
        mine = early_ref[BLK:, pl.ds(row, BLK)]
        for c in range(3):
            where_i[c] = jnp.broadcast_to(mine[c : c + 1], (BLK, BLK)).T
        total[...] = jnp.zeros_like(total)

        @pl.loop(0, chunks)
        def _(chunk):
            for half in range(CHUNK // BLK):
                theirs = where_j[chunk * (CHUNK // BLK) + half]
                gap = chunk * CHUNK + half * BLK - row
                for sub in range(0, BLK, 32):
                    square = None
                    for c in range(3):
                        delta = theirs[c : c + 1, :] - where_i[c, sub : sub + 32, :]
                        if mirrored[c]:
                            delta = theirs[c + 4 : c + 5, :] - jnp.abs(delta)
                        delta = delta * delta
                        square = delta if square is None else square + delta
                    reach = (square < 1.0) & (difference != gap - sub)
                    square = jnp.minimum(square, 1.0)
                    distance = square * lax.rsqrt(jnp.maximum(square, 1e-30))
                    envelope = jnp.full_like(square, ENVELOPE[-1])
                    for coefficient in ENVELOPE[-2::-1]:
                        envelope = envelope * square + coefficient
                    envelope = jnp.where(reach, envelope, 0.0)
                    step = gamma_width / nrbf
                    basis = envelope * jnp.exp(step * distance - gamma_width * square)
                    ratio = jnp.exp(2.0 * step * distance)
                    for k in range(nrbf):
                        if k:
                            basis = basis * ratio
                        high, low = split(basis)
                        spot = (slice(k * BLK + sub, k * BLK + sub + 32), slice(half * BLK, half * BLK + BLK))
                        high_b[spot] = high
                        low_b[spot] = low
            base = pl.multiple_of(chunk * CHUNK, CHUNK)
            ph = high_p[pl.ds(base, CHUNK), :]
            pw = low_p[pl.ds(base, CHUNK), :]
            bh = high_b[...]
            total[...] += dot(bh, ph) + (dot(bh, pw) + dot(low_b[...], ph))

        value = None
        for k in range(nrbf):
            weight = radial_ref[k : k + 1, :] * math.exp(-gamma_width * ((k + 0.5) / nrbf) ** 2)
            term = total[k * BLK : (k + 1) * BLK, :] * weight
            value = term if value is None else value + term
        message[pl.ds(row, BLK), :] = value * message_scale

    mixed = dot3(message[...], w_ref[...])
    out_ref[...] = feats_ref[...] + mixed / (1.0 + jnp.exp(-mixed))


def near_slots(sizes):
    kinds = []
    for axis, n in enumerate(sizes):
        if n == 2:
            kinds.append(("swap",))
        elif axis == 1 and n % 2 == 0:
            kinds.append(("cross", "partner"))
        else:
            kinds.append(("up", "down"))
    counts = [len(k) + 1 for k in kinds]
    slots = [(a, b, c) for a in range(counts[0]) for b in range(counts[1]) for c in range(counts[2])]
    return kinds, slots[1:]


def slot_offset(kind, index):
    side = 1 - 2 * lax.rem(index, 2)
    return {"swap": (0, 1), "cross": (-side, 0), "partner": (side, 0), "up": (-1, 0), "down": (1, 0)}[kind]


def routes(kinds):
    every = [[(axis, m) for m in range(len(kinds[axis]))] for axis in range(3)]
    first, last = every[1][:1], every[1][1:]
    return [
        [every[0], every[2], every[1]],
        [every[0], first, every[2], last],
        [every[0], every[2], every[1]],
        [first, every[2], every[0], last],
    ]


def halo_kernel(names, sizes, early_ref, later_ref, all_early, all_later, send_sem, recv_sem):
    kinds, slots = near_slots(sizes)
    width = early_ref.shape[1]
    half = width // 2
    places = [lax.axis_index(n) for n in names]

    def target(axis, m):
        n, at = sizes[axis], places[axis]
        side = 1 - 2 * lax.rem(at, 2)
        step = {"swap": 1, "cross": n - side, "partner": n + side, "up": 1, "down": n - 1}[kinds[axis][m]]
        return {names[axis]: lax.rem(at + step, n)}

    moves = [(axis, m) for axis in range(3) for m in range(len(kinds[axis]))]
    barrier = pltpu.get_barrier_semaphore()
    for move in moves:
        pl.semaphore_signal(barrier, inc=1, device_id=target(*move), device_id_type=pl.DeviceIdType.MESH)
    pl.semaphore_wait(barrier, len(moves))

    def piece(slot, number):
        own = (early_ref, later_ref)[number // 2]
        full = own if slot is None else (all_early, all_later)[number // 2].at[slot]
        return full.at[:, pl.ds(number % 2 * half, half)]

    held = [[(0, 0, 0)] for _ in range(4)]
    stages = routes(kinds)
    copies, arrived = {}, set()

    def arrive(slot, number):
        if slot != (0, 0, 0) and (slot, number) not in arrived:
            arrived.add((slot, number))
            copies[slot, number].wait_recv()

    for stage in range(max(len(r) for r in stages)):
        fresh = [[] for _ in range(4)]
        for number in range(4):
            if stage >= len(stages[number]):
                continue
            for source in held[number]:
                for axis, m in stages[number][stage]:
                    if source[axis] != 0:
                        continue
                    arrive(source, number)
                    goal = tuple(m + 1 if d == axis else source[d] for d in range(3))
                    to = slots.index(goal)
                    origin = None if source == (0, 0, 0) else slots.index(source)
                    copy = pltpu.make_async_remote_copy(
                        src_ref=piece(origin, number),
                        dst_ref=piece(to, number),
                        send_sem=send_sem.at[to, number],
                        recv_sem=recv_sem.at[to, number],
                        device_id=target(axis, m),
                        device_id_type=pl.DeviceIdType.MESH,
                    )
                    copy.start()
                    copies[goal, number] = copy
                    fresh[number].append(goal)
        for number in range(4):
            held[number] += fresh[number]
    for (slot, number), copy in copies.items():
        arrive(slot, number)
        copy.wait_send()


def local(features, positions, counts, w_src, w_out, radial):
    feats = features[0, 0, 0]
    cap, width = feats.shape
    nrbf = radial.shape[0]
    names = ("gx", "gy", "gz")
    early, later = pl.pallas_call(
        project_kernel,
        out_shape=(jax.ShapeDtypeStruct((BLK + 8, width), f32), jax.ShapeDtypeStruct((cap - BLK, width), f32)),
        in_specs=[pl.BlockSpec(memory_space=pltpu.SMEM)] + [pl.BlockSpec(memory_space=pltpu.VMEM)] * 3,
    )(counts.reshape(1), feats, positions[0, 0, 0], w_src)
    sizes = tuple(lax.axis_size(n) for n in names)
    kinds, slots = near_slots(sizes)
    near = len(slots)
    total = near + 1
    all_early, all_later = pl.pallas_call(
        lambda *refs: halo_kernel(names, sizes, *refs),
        out_shape=(jax.ShapeDtypeStruct((near, *early.shape), f32), jax.ShapeDtypeStruct((near, *later.shape), f32)),
        in_specs=[pl.BlockSpec(memory_space=pl.ANY)] * 2,
        out_specs=(pl.BlockSpec(memory_space=pl.ANY),) * 2,
        scratch_shapes=[pltpu.SemaphoreType.DMA((near, 4)), pltpu.SemaphoreType.DMA((near, 4))],
        compiler_params=pltpu.CompilerParams(collective_id=0, has_side_effects=True),
    )(early, later)
    room = total * cap + 2 * CHUNK
    out = pl.pallas_call(
        lambda *refs: pairs_kernel(names, sizes, nrbf, *refs),
        out_shape=jax.ShapeDtypeStruct((cap, width), f32),
        scratch_shapes=[
            pltpu.VMEM((room, width), bf16),
            pltpu.VMEM((room, width), bf16),
            pltpu.VMEM((room // BLK + 2, 8, BLK), f32),
            pltpu.VMEM((3, BLK, BLK), f32),
            pltpu.VMEM((nrbf * BLK, CHUNK), bf16),
            pltpu.VMEM((nrbf * BLK, CHUNK), bf16),
            pltpu.VMEM((nrbf * BLK, width), f32),
            pltpu.VMEM((cap, width), f32),
        ],
        compiler_params=pltpu.CompilerParams(vmem_limit_bytes=56 << 20),
    )(early, later, all_early, all_later, feats, radial, w_out)
    return out[None, None, None]


def solution(mesh):
    in_specs = (P("gx", "gy", "gz", None, None), P("gx", "gy", "gz", None, None), P("gx", "gy", "gz"), P(), P(), P())
    return jax.shard_map(local, mesh=mesh, in_specs=in_specs, out_specs=P("gx", "gy", "gz", None, None), check_vma=False)
```

```python
import math

import jax
import jax.numpy as jnp
import numpy as np
from jax import lax
from jax.experimental import pallas as pl
from jax.experimental.pallas import tpu as pltpu
from jax.sharding import PartitionSpec as P

BLK = 128
CHUNK = 256
PART = 32
far_value = 100.0
gamma_width = 10.0
message_scale = 0.125
highest = lax.Precision.HIGHEST
f32, bf16, i32 = jnp.float32, jnp.bfloat16, jnp.int32


def envelope_coefficients():
    t = np.cos(np.pi * (np.arange(64) + 0.5) / 64) * 0.5 + 0.5
    value = 0.5 * (np.cos(np.pi * np.sqrt(t)) + 1.0)
    fit = np.polynomial.chebyshev.Chebyshev.fit(t, value, 7, domain=[0, 1])
    return [float(c) for c in fit.convert(kind=np.polynomial.Polynomial).coef]


ENVELOPE = envelope_coefficients()


def split(value):
    high = value.astype(bf16)
    return high, (value - high.astype(f32)).astype(bf16)


def dot(a, b):
    return jnp.dot(a, b, preferred_element_type=f32)


def dot3(a, b):
    ah, al = split(a)
    bh, bl = split(b)
    return dot(ah, bh) + (dot(ah, bl) + dot(al, bh))


def project_kernel(count_ref, feats_ref, place_ref, w_ref, early_ref, later_ref):
    value = dot3(feats_ref[...], w_ref[...])
    cap = feats_ref.shape[0]
    count = count_ref[0]
    early_ref[:BLK] = value[:BLK]
    early_ref[BLK : BLK + 3] = place_ref[...]
    early_ref[BLK + 3 : BLK + 4] = jnp.broadcast_to(count.astype(f32), (1, cap))
    early_ref[BLK + 4 :] = jnp.zeros((4, cap), f32)
    later_ref[...] = value[BLK:]


def pairs_kernel(names, sizes, nrbf, *refs):
    kinds, slots = near_slots(sizes)
    tiles = len(slots) + 1
    mirrored = tuple(n == 2 for n in sizes)
    early_ref, later_ref, all_early, all_later, feats_ref, radial_ref, w_ref, out_ref = refs[:8]
    high_p, low_p, where_j, where_i, total, message, *parts = refs[8:]
    early = [early_ref] + [all_early.at[t] for t in range(tiles - 1)]
    later = [later_ref] + [all_later.at[t] for t in range(tiles - 1)]
    lane = lax.broadcasted_iota(i32, (8, BLK), 1)
    line = lax.broadcasted_iota(i32, (8, BLK), 0)
    places = [lax.axis_index(n) for n in names]

    def shift_of(t):
        shift = jnp.zeros((8, BLK), f32)
        for d in range(3):
            if t and slots[t - 1][d]:
                offset, mirror = slot_offset(kinds[d][slots[t - 1][d] - 1], places[d])
                shift = jnp.where(line == d, jnp.asarray(offset, i32).astype(f32), shift)
                shift = jnp.where(line == d + 4, float(mirror), shift)
        return shift

    counts = [jnp.max(t[BLK + 3 : BLK + 4, :BLK]).astype(i32) for t in early]
    own_blocks = (counts[0] + BLK - 1) // BLK

    def append(rows_ref, place, count, at):
        rows = (count + 15) // 16 * 16
        high, low = split(rows_ref[:BLK])
        at = pl.multiple_of(at, 16)
        high_p[pl.ds(at, BLK), :] = high
        low_p[pl.ds(at, BLK), :] = low
        turn = lax.rem(at, BLK)
        page = at // BLK
        rolled = pltpu.roll(place, turn, 1)
        where_j[page] = jnp.where(lane >= turn, rolled, where_j[page])
        where_j[page + 1] = rolled
        return at + rows

    at = jnp.int32(0)
    for half, source in ((0, early), (1, later)):
        for t in range(tiles):
            count = own_blocks * BLK if t == 0 else counts[t]
            here = jnp.clip(count - half * BLK, 0, BLK)
            place = early[t][BLK:, half * BLK : (half + 1) * BLK]
            shift = shift_of(t)
            if half:
                @pl.when(here > 0)
                def _():
                    append(source[t], place + shift, here, at)

                at = at + (here + 15) // 16 * 16
            else:
                at = append(source[t], place + shift, here, at)
            if t == 0 and half == 0:
                @pl.when(own_blocks > 1)
                def _():
                    append(later[0], early[0][BLK:, BLK:], jnp.int32(BLK), jnp.int32(BLK))

                at = own_blocks * BLK
                counts[0] = jnp.int32(0)
                own_count = own_blocks
                own_blocks = jnp.int32(0)
    own_blocks = own_count
    tail = pl.multiple_of(at, 16)
    zeros = jnp.zeros((CHUNK, high_p.shape[1]), bf16)
    high_p[pl.ds(tail, CHUNK), :] = zeros
    low_p[pl.ds(tail, CHUNK), :] = zeros
    far = jnp.where(line < 4, 2 * far_value, 0.0)
    page = at // BLK
    where_j[page] = jnp.where(lane >= lax.rem(at, BLK), far, where_j[page])
    where_j[page + 1] = far
    where_j[page + 2] = far
    chunks = (at + CHUNK - 1) // CHUNK
    difference = lax.broadcasted_iota(i32, (32, BLK), 0) - lax.broadcasted_iota(i32, (32, BLK), 1)

    message[...] = jnp.zeros_like(message)

    @pl.loop(0, own_blocks)
    def _(row_block):
        row = pl.multiple_of(row_block * BLK, BLK)
        mine = early_ref[BLK:, pl.ds(row, BLK)]
        for c in range(3):
            where_i[c] = jnp.broadcast_to(mine[c : c + 1], (BLK, BLK)).T
        total[...] = jnp.zeros_like(total)

        @pl.loop(0, chunks)
        def _(chunk):
            base = pl.multiple_of(chunk * CHUNK, CHUNK)
            pages = [where_j[chunk * (CHUNK // BLK) + half] for half in range(CHUNK // BLK)]
            for part in range(BLK // PART):
                high_b, low_b = parts[2 * part : 2 * part + 2]
                for half in range(CHUNK // BLK):
                    theirs = pages[half]
                    gap = chunk * CHUNK + half * BLK - row
                    for sub in range(0, PART, 32):
                        first = part * PART + sub
                        square = None
                        for c in range(3):
                            delta = theirs[c : c + 1, :] - where_i[c, first : first + 32, :]
                            if mirrored[c]:
                                delta = theirs[c + 4 : c + 5, :] - jnp.abs(delta)
                            delta = delta * delta
                            square = delta if square is None else square + delta
                        reach = (square < 1.0) & (difference != gap - first)
                        square = jnp.minimum(square, 1.0)
                        distance = square * lax.rsqrt(jnp.maximum(square, 1e-30))
                        envelope = jnp.full_like(square, ENVELOPE[-1])
                        for coefficient in ENVELOPE[-2::-1]:
                            envelope = envelope * square + coefficient
                        envelope = jnp.where(reach, envelope, 0.0)
                        step = gamma_width / nrbf
                        basis = envelope * jnp.exp(step * distance - gamma_width * square)
                        ratio = jnp.exp(2.0 * step * distance)
                        for k in range(nrbf):
                            if k:
                                basis = basis * ratio
                            high, low = split(basis)
                            spot = (slice(k * PART + sub, k * PART + sub + 32), slice(half * BLK, half * BLK + BLK))
                            high_b[spot] = high
                            low_b[spot] = low
                ph = high_p[pl.ds(base, CHUNK), :]
                pw = low_p[pl.ds(base, CHUNK), :]
                bh = high_b[...]
                left = jnp.concatenate([bh, bh, low_b[...]], axis=1)
                total[part] += dot(left, jnp.concatenate([ph, pw, ph], axis=0))

        for part in range(BLK // PART):
            value = None
            for k in range(nrbf):
                weight = radial_ref[k : k + 1, :] * math.exp(-gamma_width * ((k + 0.5) / nrbf) ** 2)
                term = total[part, k * PART : (k + 1) * PART, :] * weight
                value = term if value is None else value + term
            message[pl.ds(row + part * PART, PART), :] = value * message_scale

    mixed = dot3(message[...], w_ref[...])
    out_ref[...] = feats_ref[...] + mixed / (1.0 + jnp.exp(-mixed))


def near_slots(sizes):
    kinds = []
    for axis, n in enumerate(sizes):
        if n == 2:
            kinds.append(("swap",))
        elif axis == 1 and n % 2 == 0:
            kinds.append(("cross", "partner"))
        else:
            kinds.append(("up", "down"))
    counts = [len(k) + 1 for k in kinds]
    slots = [(a, b, c) for a in range(counts[0]) for b in range(counts[1]) for c in range(counts[2])]
    return kinds, slots[1:]


def slot_offset(kind, index):
    side = 1 - 2 * lax.rem(index, 2)
    return {"swap": (0, 1), "cross": (-side, 0), "partner": (side, 0), "up": (-1, 0), "down": (1, 0)}[kind]


def routes(kinds):
    every = [[(axis, m) for m in range(len(kinds[axis]))] for axis in range(3)]
    first, last = every[1][:1], every[1][1:]
    return [
        [every[0], every[2], every[1]],
        [every[0], first, every[2], last],
        [every[0], every[2], every[1]],
        [first, every[2], every[0], last],
    ]


def halo_kernel(names, sizes, early_ref, later_ref, all_early, all_later, send_sem, recv_sem):
    kinds, slots = near_slots(sizes)
    width = early_ref.shape[1]
    half = width // 2
    places = [lax.axis_index(n) for n in names]

    def target(axis, m):
        n, at = sizes[axis], places[axis]
        side = 1 - 2 * lax.rem(at, 2)
        step = {"swap": 1, "cross": n - side, "partner": n + side, "up": 1, "down": n - 1}[kinds[axis][m]]
        return {names[axis]: lax.rem(at + step, n)}

    moves = [(axis, m) for axis in range(3) for m in range(len(kinds[axis]))]
    barrier = pltpu.get_barrier_semaphore()
    for move in moves:
        pl.semaphore_signal(barrier, inc=1, device_id=target(*move), device_id_type=pl.DeviceIdType.MESH)
    pl.semaphore_wait(barrier, len(moves))

    def piece(slot, number):
        own = (early_ref, later_ref)[number // 2]
        full = own if slot is None else (all_early, all_later)[number // 2].at[slot]
        return full.at[:, pl.ds(number % 2 * half, half)]

    plan = []
    for number, route in enumerate(routes(kinds)):
        held = [((0, 0, 0), 0)]
        for stage, moved in enumerate(route):
            fresh = []
            for source, depth in held:
                for axis, m in moved:
                    if source[axis] == 0:
                        goal = tuple(m + 1 if d == axis else source[d] for d in range(3))
                        plan.append((depth, stage, number, source, goal, axis, m))
                        fresh.append((goal, depth + 1))
            held += fresh
    copies, arrived = {}, set()

    def arrive(slot, number):
        if slot != (0, 0, 0) and (slot, number) not in arrived:
            arrived.add((slot, number))
            copies[slot, number].wait_recv()

    for _, _, number, source, goal, axis, m in sorted(plan, key=lambda p: p[:3]):
        arrive(source, number)
        to = slots.index(goal)
        origin = None if source == (0, 0, 0) else slots.index(source)
        copy = pltpu.make_async_remote_copy(
            src_ref=piece(origin, number),
            dst_ref=piece(to, number),
            send_sem=send_sem.at[to, number],
            recv_sem=recv_sem.at[to, number],
            device_id=target(axis, m),
            device_id_type=pl.DeviceIdType.MESH,
        )
        copy.start()
        copies[goal, number] = copy
    for (slot, number), copy in copies.items():
        arrive(slot, number)
        copy.wait_send()


def local(features, positions, counts, w_src, w_out, radial):
    feats = features[0, 0, 0]
    cap, width = feats.shape
    nrbf = radial.shape[0]
    slot = lax.broadcasted_iota(i32, (1, cap), 1)
    placed = jnp.where(slot < counts[0, 0, 0], positions[0, 0, 0], far_value)
    names = ("gx", "gy", "gz")
    early, later = pl.pallas_call(
        project_kernel,
        out_shape=(jax.ShapeDtypeStruct((BLK + 8, width), f32), jax.ShapeDtypeStruct((cap - BLK, width), f32)),
        in_specs=[pl.BlockSpec(memory_space=pltpu.SMEM)] + [pl.BlockSpec(memory_space=pltpu.VMEM)] * 3,
    )(counts.reshape(1), feats, placed, w_src)
    sizes = tuple(lax.axis_size(n) for n in names)
    kinds, slots = near_slots(sizes)
    near = len(slots)
    total = near + 1
    all_early, all_later = pl.pallas_call(
        lambda *refs: halo_kernel(names, sizes, *refs),
        out_shape=(jax.ShapeDtypeStruct((near, *early.shape), f32), jax.ShapeDtypeStruct((near, *later.shape), f32)),
        in_specs=[pl.BlockSpec(memory_space=pl.ANY)] * 2,
        out_specs=(pl.BlockSpec(memory_space=pl.ANY),) * 2,
        scratch_shapes=[pltpu.SemaphoreType.DMA((near, 4)), pltpu.SemaphoreType.DMA((near, 4))],
        compiler_params=pltpu.CompilerParams(collective_id=0, has_side_effects=True),
    )(early, later)
    room = total * cap + 2 * CHUNK
    out = pl.pallas_call(
        lambda *refs: pairs_kernel(names, sizes, nrbf, *refs),
        out_shape=jax.ShapeDtypeStruct((cap, width), f32),
        scratch_shapes=[
            pltpu.VMEM((room, width), bf16),
            pltpu.VMEM((room, width), bf16),
            pltpu.VMEM((room // BLK + 2, 8, BLK), f32),
            pltpu.VMEM((3, BLK, BLK), f32),
            pltpu.VMEM((BLK // PART, nrbf * PART, width), f32),
            pltpu.VMEM((cap, width), f32),
            *[pltpu.VMEM((nrbf * PART, CHUNK), bf16) for _ in range(2 * (BLK // PART))],
        ],
        compiler_params=pltpu.CompilerParams(vmem_limit_bytes=56 << 20),
    )(early, later, all_early, all_later, feats, radial, w_out)
    return out[None, None, None]


def solution(mesh):
    in_specs = (P("gx", "gy", "gz", None, None), P("gx", "gy", "gz", None, None), P("gx", "gy", "gz"), P(), P(), P())
    return jax.shard_map(local, mesh=mesh, in_specs=in_specs, out_specs=P("gx", "gy", "gz", None, None), check_vma=False)
```

```python
import math

import jax
import jax.numpy as jnp
import numpy as np
from jax import lax
from jax.experimental import pallas as pl
from jax.experimental.pallas import tpu as pltpu
from jax.sharding import PartitionSpec as P

BLK = 128
CHUNK = 256
PART = 32
far_value = 100.0
gamma_width = 10.0
message_scale = 0.125
highest = lax.Precision.HIGHEST
f32, bf16, i32 = jnp.float32, jnp.bfloat16, jnp.int32


def envelope_coefficients():
    t = np.cos(np.pi * (np.arange(64) + 0.5) / 64) * 0.5 + 0.5
    value = 0.5 * (np.cos(np.pi * np.sqrt(t)) + 1.0)
    fit = np.polynomial.chebyshev.Chebyshev.fit(t, value, 7, domain=[0, 1])
    return [float(c) for c in fit.convert(kind=np.polynomial.Polynomial).coef]


ENVELOPE = envelope_coefficients()


def split(value):
    high = value.astype(bf16)
    return high, (value - high.astype(f32)).astype(bf16)


def dot(a, b):
    return jnp.dot(a, b, preferred_element_type=f32)


def dot3(a, b):
    ah, al = split(a)
    bh, bl = split(b)
    return dot(ah, bh) + (dot(ah, bl) + dot(al, bh))


def project_kernel(count_ref, feats_ref, place_ref, w_ref, early_ref, later_ref):
    value = dot3(feats_ref[...], w_ref[...])
    cap = feats_ref.shape[0]
    count = count_ref[0]
    early_ref[:BLK] = value[:BLK]
    slot = lax.broadcasted_iota(i32, (1, cap), 1)
    for d in range(3):
        early_ref[BLK + d : BLK + d + 1] = jnp.where(slot < count, place_ref[:, d * cap : (d + 1) * cap], far_value)
    early_ref[BLK + 3 : BLK + 4] = jnp.broadcast_to(count.astype(f32), (1, cap))
    early_ref[BLK + 4 :] = jnp.zeros((4, cap), f32)
    later_ref[...] = value[BLK:]


def pairs_kernel(names, sizes, nrbf, *refs):
    kinds, slots = near_slots(sizes)
    tiles = len(slots) + 1
    mirrored = tuple(n == 2 for n in sizes)
    early_ref, later_ref, all_early, all_later, feats_ref, radial_ref, w_ref, out_ref = refs[:8]
    high_p, low_p, where_j, where_i, total, message, *parts = refs[8:]
    early = [early_ref] + [all_early.at[t] for t in range(tiles - 1)]
    later = [later_ref] + [all_later.at[t] for t in range(tiles - 1)]
    lane = lax.broadcasted_iota(i32, (8, BLK), 1)
    line = lax.broadcasted_iota(i32, (8, BLK), 0)
    places = [lax.axis_index(n) for n in names]

    def shift_of(t):
        shift = jnp.zeros((8, BLK), f32)
        for d in range(3):
            if t and slots[t - 1][d]:
                offset, mirror = slot_offset(kinds[d][slots[t - 1][d] - 1], places[d])
                shift = jnp.where(line == d, jnp.asarray(offset, i32).astype(f32), shift)
                shift = jnp.where(line == d + 4, float(mirror), shift)
        return shift

    counts = [jnp.max(t[BLK + 3 : BLK + 4, :BLK]).astype(i32) for t in early]
    own_blocks = (counts[0] + BLK - 1) // BLK

    def append(rows_ref, place, count, at):
        rows = (count + 15) // 16 * 16
        high, low = split(rows_ref[:BLK])
        at = pl.multiple_of(at, 16)
        high_p[pl.ds(at, BLK), :] = high
        low_p[pl.ds(at, BLK), :] = low
        turn = lax.rem(at, BLK)
        page = at // BLK
        rolled = pltpu.roll(place, turn, 1)
        where_j[page] = jnp.where(lane >= turn, rolled, where_j[page])
        where_j[page + 1] = rolled
        return at + rows

    at = jnp.int32(0)
    for half, source in ((0, early), (1, later)):
        for t in range(tiles):
            count = own_blocks * BLK if t == 0 else counts[t]
            here = jnp.clip(count - half * BLK, 0, BLK)
            place = early[t][BLK:, half * BLK : (half + 1) * BLK]
            shift = shift_of(t)
            if half:
                @pl.when(here > 0)
                def _():
                    append(source[t], place + shift, here, at)

                at = at + (here + 15) // 16 * 16
            else:
                at = append(source[t], place + shift, here, at)
            if t == 0 and half == 0:
                @pl.when(own_blocks > 1)
                def _():
                    append(later[0], early[0][BLK:, BLK:], jnp.int32(BLK), jnp.int32(BLK))

                at = own_blocks * BLK
                counts[0] = jnp.int32(0)
                own_count = own_blocks
                own_blocks = jnp.int32(0)
    own_blocks = own_count
    tail = pl.multiple_of(at, 16)
    zeros = jnp.zeros((CHUNK, high_p.shape[1]), bf16)
    high_p[pl.ds(tail, CHUNK), :] = zeros
    low_p[pl.ds(tail, CHUNK), :] = zeros
    far = jnp.where(line < 4, 2 * far_value, 0.0)
    page = at // BLK
    where_j[page] = jnp.where(lane >= lax.rem(at, BLK), far, where_j[page])
    where_j[page + 1] = far
    where_j[page + 2] = far
    chunks = (at + CHUNK - 1) // CHUNK
    difference = lax.broadcasted_iota(i32, (32, BLK), 0) - lax.broadcasted_iota(i32, (32, BLK), 1)

    message[...] = jnp.zeros_like(message)

    @pl.loop(0, own_blocks)
    def _(row_block):
        row = pl.multiple_of(row_block * BLK, BLK)
        mine = early_ref[BLK:, pl.ds(row, BLK)]
        for c in range(3):
            where_i[c] = jnp.broadcast_to(mine[c : c + 1], (BLK, BLK)).T
        total[...] = jnp.zeros_like(total)

        @pl.loop(0, chunks)
        def _(chunk):
            base = pl.multiple_of(chunk * CHUNK, CHUNK)
            pages = [where_j[chunk * (CHUNK // BLK) + half] for half in range(CHUNK // BLK)]
            for part in range(BLK // PART):
                high_b, low_b = parts[2 * part : 2 * part + 2]
                for half in range(CHUNK // BLK):
                    theirs = pages[half]
                    gap = chunk * CHUNK + half * BLK - row
                    for sub in range(0, PART, 32):
                        first = part * PART + sub
                        square = None
                        for c in range(3):
                            delta = theirs[c : c + 1, :] - where_i[c, first : first + 32, :]
                            if mirrored[c]:
                                delta = theirs[c + 4 : c + 5, :] - jnp.abs(delta)
                            delta = delta * delta
                            square = delta if square is None else square + delta
                        reach = (square < 1.0) & (difference != gap - first)
                        square = jnp.minimum(square, 1.0)
                        distance = square * lax.rsqrt(jnp.maximum(square, 1e-30))
                        envelope = jnp.full_like(square, ENVELOPE[-1])
                        for coefficient in ENVELOPE[-2::-1]:
                            envelope = envelope * square + coefficient
                        envelope = jnp.where(reach, envelope, 0.0)
                        step = gamma_width / nrbf
                        basis = envelope * jnp.exp(step * distance - gamma_width * square)
                        ratio = jnp.exp(2.0 * step * distance)
                        for k in range(nrbf):
                            if k:
                                basis = basis * ratio
                            high, low = split(basis)
                            spot = (slice(k * PART + sub, k * PART + sub + 32), slice(half * BLK, half * BLK + BLK))
                            high_b[spot] = high
                            low_b[spot] = low
                ph = high_p[pl.ds(base, CHUNK), :]
                pw = low_p[pl.ds(base, CHUNK), :]
                bh = high_b[...]
                left = jnp.concatenate([bh, bh, low_b[...]], axis=1)
                total[part] += dot(left, jnp.concatenate([ph, pw, ph], axis=0))

        for part in range(BLK // PART):
            value = None
            for k in range(nrbf):
                weight = radial_ref[k : k + 1, :] * math.exp(-gamma_width * ((k + 0.5) / nrbf) ** 2)
                term = total[part, k * PART : (k + 1) * PART, :] * weight
                value = term if value is None else value + term
            message[pl.ds(row + part * PART, PART), :] = value * message_scale

    mixed = dot3(message[...], w_ref[...])
    out_ref[...] = feats_ref[...] + mixed / (1.0 + jnp.exp(-mixed))


def near_slots(sizes):
    kinds = []
    for axis, n in enumerate(sizes):
        if n == 2:
            kinds.append(("swap",))
        elif axis == 1 and n % 2 == 0:
            kinds.append(("cross", "partner"))
        else:
            kinds.append(("up", "down"))
    counts = [len(k) + 1 for k in kinds]
    slots = [(a, b, c) for a in range(counts[0]) for b in range(counts[1]) for c in range(counts[2])]
    return kinds, slots[1:]


def slot_offset(kind, index):
    side = 1 - 2 * lax.rem(index, 2)
    return {"swap": (0, 1), "cross": (-side, 0), "partner": (side, 0), "up": (-1, 0), "down": (1, 0)}[kind]


def routes(kinds):
    every = [[(axis, m) for m in range(len(kinds[axis]))] for axis in range(3)]
    first, last = every[1][:1], every[1][1:]
    return [
        [first, every[2], every[0], last],
        [every[0], first, every[2], last],
        [every[0], every[2], every[1]],
        [every[0], every[2], every[1]],
    ]


def halo_kernel(names, sizes, early_ref, later_ref, all_early, all_later, send_sem, recv_sem):
    kinds, slots = near_slots(sizes)
    width = early_ref.shape[1]
    half = width // 2
    places = [lax.axis_index(n) for n in names]

    def target(axis, m):
        n, at = sizes[axis], places[axis]
        side = 1 - 2 * lax.rem(at, 2)
        step = {"swap": 1, "cross": n - side, "partner": n + side, "up": 1, "down": n - 1}[kinds[axis][m]]
        return {names[axis]: lax.rem(at + step, n)}

    moves = [(axis, m) for axis in range(3) for m in range(len(kinds[axis]))]
    barrier = pltpu.get_barrier_semaphore()
    for move in moves:
        pl.semaphore_signal(barrier, inc=1, device_id=target(*move), device_id_type=pl.DeviceIdType.MESH)
    pl.semaphore_wait(barrier, len(moves))

    def piece(slot, number):
        own = (early_ref, later_ref)[number // 2]
        full = own if slot is None else (all_early, all_later)[number // 2].at[slot]
        return full.at[:, pl.ds(number % 2 * half, half)]

    plan = []
    for number, route in enumerate(routes(kinds)):
        held = [((0, 0, 0), 0)]
        for stage, moved in enumerate(route):
            fresh = []
            for source, depth in held:
                for axis, m in moved:
                    if source[axis] == 0:
                        goal = tuple(m + 1 if d == axis else source[d] for d in range(3))
                        plan.append((depth, stage, number, source, goal, axis, m))
                        fresh.append((goal, depth + 1))
            held += fresh
    copies, arrived = {}, set()

    def arrive(slot, number):
        if slot != (0, 0, 0) and (slot, number) not in arrived:
            arrived.add((slot, number))
            copies[slot, number].wait_recv()

    for _, _, number, source, goal, axis, m in sorted(plan, key=lambda p: (p[5:] == (1, 1), *p[:3])):
        arrive(source, number)
        to = slots.index(goal)
        origin = None if source == (0, 0, 0) else slots.index(source)
        copy = pltpu.make_async_remote_copy(
            src_ref=piece(origin, number),
            dst_ref=piece(to, number),
            send_sem=send_sem.at[to, number],
            recv_sem=recv_sem.at[to, number],
            device_id=target(axis, m),
            device_id_type=pl.DeviceIdType.MESH,
        )
        copy.start()
        copies[goal, number] = copy
    for (slot, number), copy in copies.items():
        arrive(slot, number)
        copy.wait_send()


def local(features, positions, counts, w_src, w_out, radial):
    feats = features[0, 0, 0]
    cap, width = feats.shape
    nrbf = radial.shape[0]
    names = ("gx", "gy", "gz")
    early, later = pl.pallas_call(
        project_kernel,
        out_shape=(jax.ShapeDtypeStruct((BLK + 8, width), f32), jax.ShapeDtypeStruct((cap - BLK, width), f32)),
        in_specs=[pl.BlockSpec(memory_space=pltpu.SMEM)] + [pl.BlockSpec(memory_space=pltpu.VMEM)] * 3,
    )(counts.reshape(1), feats, positions.reshape(1, -1), w_src)
    sizes = tuple(lax.axis_size(n) for n in names)
    kinds, slots = near_slots(sizes)
    near = len(slots)
    total = near + 1
    all_early, all_later = pl.pallas_call(
        lambda *refs: halo_kernel(names, sizes, *refs),
        out_shape=(jax.ShapeDtypeStruct((near, *early.shape), f32), jax.ShapeDtypeStruct((near, *later.shape), f32)),
        in_specs=[pl.BlockSpec(memory_space=pl.ANY)] * 2,
        out_specs=(pl.BlockSpec(memory_space=pl.ANY),) * 2,
        scratch_shapes=[pltpu.SemaphoreType.DMA((near, 4)), pltpu.SemaphoreType.DMA((near, 4))],
        compiler_params=pltpu.CompilerParams(collective_id=0, has_side_effects=True),
    )(early, later)
    room = total * cap + 2 * CHUNK
    out = pl.pallas_call(
        lambda *refs: pairs_kernel(names, sizes, nrbf, *refs),
        out_shape=jax.ShapeDtypeStruct((cap, width), f32),
        scratch_shapes=[
            pltpu.VMEM((room, width), bf16),
            pltpu.VMEM((room, width), bf16),
            pltpu.VMEM((room // BLK + 2, 8, BLK), f32),
            pltpu.VMEM((3, BLK, BLK), f32),
            pltpu.VMEM((BLK // PART, nrbf * PART, width), f32),
            pltpu.VMEM((cap, width), f32),
            *[pltpu.VMEM((nrbf * PART, CHUNK), bf16) for _ in range(2 * (BLK // PART))],
        ],
        compiler_params=pltpu.CompilerParams(vmem_limit_bytes=56 << 20),
    )(early, later, all_early, all_later, feats, radial, w_out)
    return out[None, None, None]


def solution(mesh):
    in_specs = (P("gx", "gy", "gz", None, None), P("gx", "gy", "gz", None, None), P("gx", "gy", "gz"), P(), P(), P())
    return jax.shard_map(local, mesh=mesh, in_specs=in_specs, out_specs=P("gx", "gy", "gz", None, None), check_vma=False)
```

```python
import math

import jax
import jax.numpy as jnp
import numpy as np
from jax import lax
from jax.experimental import pallas as pl
from jax.experimental.pallas import tpu as pltpu
from jax.sharding import PartitionSpec as P

BLK = 128
CHUNK = 256
PART = 16
far_value = 100.0
gamma_width = 10.0
message_scale = 0.125
highest = lax.Precision.HIGHEST
f32, bf16, i32 = jnp.float32, jnp.bfloat16, jnp.int32


def envelope_coefficients():
    t = np.cos(np.pi * (np.arange(64) + 0.5) / 64) * 0.5 + 0.5
    value = 0.5 * (np.cos(np.pi * np.sqrt(t)) + 1.0)
    fit = np.polynomial.chebyshev.Chebyshev.fit(t, value, 7, domain=[0, 1])
    return [float(c) for c in fit.convert(kind=np.polynomial.Polynomial).coef]


ENVELOPE = envelope_coefficients()


def split(value):
    high = value.astype(bf16)
    return high, (value - high.astype(f32)).astype(bf16)


def dot(a, b):
    return jnp.dot(a, b, preferred_element_type=f32)


def dot3(a, b):
    ah, al = split(a)
    bh, bl = split(b)
    return dot(ah, bh) + (dot(ah, bl) + dot(al, bh))


def project_kernel(count_ref, feats_ref, place_ref, w_ref, early_ref, later_ref):
    value = dot3(feats_ref[...], w_ref[...])
    cap = feats_ref.shape[0]
    count = count_ref[0]
    early_ref[:BLK] = value[:BLK]
    slot = lax.broadcasted_iota(i32, (1, cap), 1)
    for d in range(3):
        early_ref[BLK + d : BLK + d + 1] = jnp.where(slot < count, place_ref[:, d * cap : (d + 1) * cap], far_value)
    early_ref[BLK + 3 : BLK + 4] = jnp.broadcast_to(count.astype(f32), (1, cap))
    early_ref[BLK + 4 :] = jnp.zeros((4, cap), f32)
    later_ref[...] = value[BLK:]


def pairs_kernel(names, sizes, nrbf, *refs):
    kinds, slots = near_slots(sizes)
    tiles = len(slots) + 1
    mirrored = tuple(n == 2 for n in sizes)
    early_ref, later_ref, all_early, all_later, feats_ref, radial_ref, w_ref, out_ref = refs[:8]
    high_p, low_p, where_j, where_i, total, message, *parts = refs[8:]
    early = [early_ref] + [all_early.at[t] for t in range(tiles - 1)]
    later = [later_ref] + [all_later.at[t] for t in range(tiles - 1)]
    lane = lax.broadcasted_iota(i32, (8, BLK), 1)
    line = lax.broadcasted_iota(i32, (8, BLK), 0)
    places = [lax.axis_index(n) for n in names]

    def shift_of(t):
        shift = jnp.zeros((8, BLK), f32)
        for d in range(3):
            if t and slots[t - 1][d]:
                offset, mirror = slot_offset(kinds[d][slots[t - 1][d] - 1], places[d])
                shift = jnp.where(line == d, jnp.asarray(offset, i32).astype(f32), shift)
                shift = jnp.where(line == d + 4, float(mirror), shift)
        return shift

    counts = [jnp.max(t[BLK + 3 : BLK + 4, :BLK]).astype(i32) for t in early]
    own_blocks = (counts[0] + BLK - 1) // BLK

    def append(rows_ref, place, count, at):
        rows = (count + 15) // 16 * 16
        high, low = split(rows_ref[:BLK])
        at = pl.multiple_of(at, 16)
        high_p[pl.ds(at, BLK), :] = high
        low_p[pl.ds(at, BLK), :] = low
        turn = lax.rem(at, BLK)
        page = at // BLK
        rolled = pltpu.roll(place, turn, 1)
        where_j[page] = jnp.where(lane >= turn, rolled, where_j[page])
        where_j[page + 1] = rolled
        return at + rows

    at = jnp.int32(0)
    for half, source in ((0, early), (1, later)):
        for t in range(tiles):
            count = own_blocks * BLK if t == 0 else counts[t]
            here = jnp.clip(count - half * BLK, 0, BLK)
            place = early[t][BLK:, half * BLK : (half + 1) * BLK]
            shift = shift_of(t)
            if half:
                @pl.when(here > 0)
                def _():
                    append(source[t], place + shift, here, at)

                at = at + (here + 15) // 16 * 16
            else:
                at = append(source[t], place + shift, here, at)
            if t == 0 and half == 0:
                @pl.when(own_blocks > 1)
                def _():
                    append(later[0], early[0][BLK:, BLK:], jnp.int32(BLK), jnp.int32(BLK))

                at = own_blocks * BLK
                counts[0] = jnp.int32(0)
                own_count = own_blocks
                own_blocks = jnp.int32(0)
    own_blocks = own_count
    tail = pl.multiple_of(at, 16)
    zeros = jnp.zeros((CHUNK, high_p.shape[1]), bf16)
    high_p[pl.ds(tail, CHUNK), :] = zeros
    low_p[pl.ds(tail, CHUNK), :] = zeros
    far = jnp.where(line < 4, 2 * far_value, 0.0)
    page = at // BLK
    where_j[page] = jnp.where(lane >= lax.rem(at, BLK), far, where_j[page])
    where_j[page + 1] = far
    where_j[page + 2] = far
    chunks = (at + CHUNK - 1) // CHUNK
    difference = lax.broadcasted_iota(i32, (16, BLK), 0) - lax.broadcasted_iota(i32, (16, BLK), 1)

    message[...] = jnp.zeros_like(message)

    @pl.loop(0, own_blocks)
    def _(row_block):
        row = pl.multiple_of(row_block * BLK, BLK)
        mine = early_ref[BLK:, pl.ds(row, BLK)]
        for c in range(3):
            where_i[c] = jnp.broadcast_to(mine[c : c + 1], (BLK, BLK)).T
        total[...] = jnp.zeros_like(total)

        @pl.loop(0, chunks)
        def _(chunk):
            base = pl.multiple_of(chunk * CHUNK, CHUNK)
            pages = [where_j[chunk * (CHUNK // BLK) + half] for half in range(CHUNK // BLK)]
            for part in range(BLK // PART):
                high_b, low_b = parts[2 * part : 2 * part + 2]
                for half in range(CHUNK // BLK):
                    theirs = pages[half]
                    gap = chunk * CHUNK + half * BLK - row
                    for sub in range(0, PART, 16):
                        first = part * PART + sub
                        square = None
                        for c in range(3):
                            delta = theirs[c : c + 1, :] - where_i[c, first : first + 16, :]
                            if mirrored[c]:
                                delta = theirs[c + 4 : c + 5, :] - jnp.abs(delta)
                            delta = delta * delta
                            square = delta if square is None else square + delta
                        reach = (square < 1.0) & (difference != gap - first)
                        square = jnp.minimum(square, 1.0)
                        distance = square * lax.rsqrt(jnp.maximum(square, 1e-30))
                        envelope = jnp.full_like(square, ENVELOPE[-1])
                        for coefficient in ENVELOPE[-2::-1]:
                            envelope = envelope * square + coefficient
                        envelope = jnp.where(reach, envelope, 0.0)
                        step = gamma_width / nrbf
                        basis = envelope * jnp.exp(step * distance - gamma_width * square)
                        ratio = jnp.exp(2.0 * step * distance)
                        for k in range(nrbf):
                            if k:
                                basis = basis * ratio
                            high, low = split(basis)
                            spot = (slice(k * PART + sub, k * PART + sub + 16), slice(half * BLK, half * BLK + BLK))
                            high_b[spot] = high
                            low_b[spot] = low
                ph = high_p[pl.ds(base, CHUNK), :]
                pw = low_p[pl.ds(base, CHUNK), :]
                bh = high_b[...]
                left = jnp.concatenate([bh, bh, low_b[...]], axis=1)
                total[part] += dot(left, jnp.concatenate([ph, pw, ph], axis=0))

        for part in range(BLK // PART):
            value = None
            for k in range(nrbf):
                weight = radial_ref[k : k + 1, :] * math.exp(-gamma_width * ((k + 0.5) / nrbf) ** 2)
                term = total[part, k * PART : (k + 1) * PART, :] * weight
                value = term if value is None else value + term
            message[pl.ds(row + part * PART, PART), :] = value * message_scale

    mixed = dot3(message[...], w_ref[...])
    out_ref[...] = feats_ref[...] + mixed / (1.0 + jnp.exp(-mixed))


def near_slots(sizes):
    kinds = []
    for axis, n in enumerate(sizes):
        if n == 2:
            kinds.append(("swap",))
        elif axis == 1 and n % 2 == 0:
            kinds.append(("cross", "partner"))
        else:
            kinds.append(("up", "down"))
    counts = [len(k) + 1 for k in kinds]
    slots = [(a, b, c) for a in range(counts[0]) for b in range(counts[1]) for c in range(counts[2])]
    return kinds, slots[1:]


def slot_offset(kind, index):
    side = 1 - 2 * lax.rem(index, 2)
    return {"swap": (0, 1), "cross": (-side, 0), "partner": (side, 0), "up": (-1, 0), "down": (1, 0)}[kind]


def routes(kinds):
    every = [[(axis, m) for m in range(len(kinds[axis]))] for axis in range(3)]
    first, last = every[1][:1], every[1][1:]
    return [
        [first, every[2], every[0], last],
        [every[0], first, every[2], last],
        [every[0], every[2], every[1]],
        [every[0], every[2], every[1]],
    ]


def halo_kernel(names, sizes, early_ref, later_ref, all_early, all_later, send_sem, recv_sem):
    kinds, slots = near_slots(sizes)
    width = early_ref.shape[1]
    half = width // 2
    places = [lax.axis_index(n) for n in names]

    def target(axis, m):
        n, at = sizes[axis], places[axis]
        side = 1 - 2 * lax.rem(at, 2)
        step = {"swap": 1, "cross": n - side, "partner": n + side, "up": 1, "down": n - 1}[kinds[axis][m]]
        return {names[axis]: lax.rem(at + step, n)}

    moves = [(axis, m) for axis in range(3) for m in range(len(kinds[axis]))]
    barrier = pltpu.get_barrier_semaphore()
    for move in moves:
        pl.semaphore_signal(barrier, inc=1, device_id=target(*move), device_id_type=pl.DeviceIdType.MESH)
    pl.semaphore_wait(barrier, len(moves))

    def piece(slot, number):
        own = (early_ref, later_ref)[number // 2]
        full = own if slot is None else (all_early, all_later)[number // 2].at[slot]
        return full.at[:, pl.ds(number % 2 * half, half)]

    plan = []
    for number, route in enumerate(routes(kinds)):
        held = [((0, 0, 0), 0)]
        for stage, moved in enumerate(route):
            fresh = []
            for source, depth in held:
                for axis, m in moved:
                    if source[axis] == 0:
                        goal = tuple(m + 1 if d == axis else source[d] for d in range(3))
                        plan.append((depth, stage, number, source, goal, axis, m))
                        fresh.append((goal, depth + 1))
            held += fresh
    copies, arrived = {}, set()

    def arrive(slot, number):
        if slot != (0, 0, 0) and (slot, number) not in arrived:
            arrived.add((slot, number))
            copies[slot, number].wait_recv()

    for _, _, number, source, goal, axis, m in sorted(plan, key=lambda p: (p[5:] == (1, 1), *p[:3])):
        arrive(source, number)
        to = slots.index(goal)
        origin = None if source == (0, 0, 0) else slots.index(source)
        copy = pltpu.make_async_remote_copy(
            src_ref=piece(origin, number),
            dst_ref=piece(to, number),
            send_sem=send_sem.at[to, number],
            recv_sem=recv_sem.at[to, number],
            device_id=target(axis, m),
            device_id_type=pl.DeviceIdType.MESH,
        )
        copy.start()
        copies[goal, number] = copy
    for (slot, number), copy in copies.items():
        arrive(slot, number)
        copy.wait_send()


def local(features, positions, counts, w_src, w_out, radial):
    feats = features[0, 0, 0]
    cap, width = feats.shape
    nrbf = radial.shape[0]
    names = ("gx", "gy", "gz")
    early, later = pl.pallas_call(
        project_kernel,
        out_shape=(jax.ShapeDtypeStruct((BLK + 8, width), f32), jax.ShapeDtypeStruct((cap - BLK, width), f32)),
        in_specs=[pl.BlockSpec(memory_space=pltpu.SMEM)] + [pl.BlockSpec(memory_space=pltpu.VMEM)] * 3,
    )(counts.reshape(1), feats, positions.reshape(1, -1), w_src)
    sizes = tuple(lax.axis_size(n) for n in names)
    kinds, slots = near_slots(sizes)
    near = len(slots)
    total = near + 1
    all_early, all_later = pl.pallas_call(
        lambda *refs: halo_kernel(names, sizes, *refs),
        out_shape=(jax.ShapeDtypeStruct((near, *early.shape), f32), jax.ShapeDtypeStruct((near, *later.shape), f32)),
        in_specs=[pl.BlockSpec(memory_space=pl.ANY)] * 2,
        out_specs=(pl.BlockSpec(memory_space=pl.ANY),) * 2,
        scratch_shapes=[pltpu.SemaphoreType.DMA((near, 4)), pltpu.SemaphoreType.DMA((near, 4))],
        compiler_params=pltpu.CompilerParams(collective_id=0, has_side_effects=True),
    )(early, later)
    room = total * cap + 2 * CHUNK
    out = pl.pallas_call(
        lambda *refs: pairs_kernel(names, sizes, nrbf, *refs),
        out_shape=jax.ShapeDtypeStruct((cap, width), f32),
        scratch_shapes=[
            pltpu.VMEM((room, width), bf16),
            pltpu.VMEM((room, width), bf16),
            pltpu.VMEM((room // BLK + 2, 8, BLK), f32),
            pltpu.VMEM((3, BLK, BLK), f32),
            pltpu.VMEM((BLK // PART, nrbf * PART, width), f32),
            pltpu.VMEM((cap, width), f32),
            *[pltpu.VMEM((nrbf * PART, CHUNK), bf16) for _ in range(2 * (BLK // PART))],
        ],
        compiler_params=pltpu.CompilerParams(vmem_limit_bytes=56 << 20),
    )(early, later, all_early, all_later, feats, radial, w_out)
    return out[None, None, None]


def solution(mesh):
    in_specs = (P("gx", "gy", "gz", None, None), P("gx", "gy", "gz", None, None), P("gx", "gy", "gz"), P(), P(), P())
    return jax.shard_map(local, mesh=mesh, in_specs=in_specs, out_specs=P("gx", "gy", "gz", None, None), check_vma=False)
```
